32 devices in a mesh: sph: 8 (over z, x), ang: 4 (over y, core).
Axes of the slice: x: 2, y: 2, z: 4, core: 2. Of those that a mesh axis runs over, the one named last changes fastest.
Arguments:
- coefficients: bfloat16 [256, 240, 1024], P(('sph', 'ang')), may hold values from -0.039794922 to 0.039794922
- positions: int32 [256, 3], P(('sph', 'ang')), may hold values from 0 to 7
- shift_tables: bfloat16 [3, 8, 480, 240], replicated, may hold values from -1.3 to 1.3
- absorb_weight: float32 [256, 240], P(('sph', 'ang')), may hold values from 0.02 to 0.9, as said below
- incident: float32 [240, 1024], replicated, may hold values from -1.6 to 1.6
- detector: float32 [32, 64], P('sph'), may hold values from 0.002 to 0.18, as said below
Outputs:
- amplitude: float32 [2, 2, 32, 64, 512], P(None, None, 'sph', 'ang')
- cross_sections: float32 [3, 512], P(None, 'ang')
The draws below stay inside these ranges and needn't reach their ends.
Inputs may be any that keep to these rules, and one draw needn't show every extreme that they name: `absorb_weight`: Positive. `detector`: Positive.
All inputs are finite; a program needn't handle non-finite values.
Results may differ from the reference program's by a relative error of at most 0.0003.
The reference program's roundings to bfloat16 on the way (of `first` and `second`) count: a program that leaves them out, or rounds other values in their place, can miss the bound.
Values sent between devices are 32-bit elements; how exact they have to be, the bound alone decides.
A program may use at most 128 MiB of HBM per device.

```python
import math
import jax
import jax.numpy as jnp
from jax import lax

ORDER = 10
NCOEF = 240
AZIM = 64
GRID = 8
SPH_DEV = 8
FIELDS = 512
SPHERES = 256
POLAR = 32


def draw_shift_tables(key, part):
    diag_key = jax.random.fold_in(key, 11)
    noise_key = jax.random.fold_in(key, 12)
    diagonal = jax.random.uniform(diag_key, (3, GRID, NCOEF), jnp.float32, 0.7, 1.3)
    spread = 0.3 / math.sqrt(NCOEF)
    noise = jnp.clip(jax.random.normal(noise_key, (3, GRID, 2 * NCOEF, NCOEF), jnp.float32), -4.0, 4.0) * spread
    identity = jnp.eye(NCOEF, dtype=jnp.float32)
    real_block = noise[:, :, :NCOEF, :] * (1.0 - identity) + diagonal[:, :, :, None] * identity
    return jnp.concatenate([real_block, noise[:, :, NCOEF:, :]], axis=2).astype(jnp.bfloat16)


def draw_absorb_weight(key, part):
    rate = jnp.exp(jax.random.uniform(jax.random.fold_in(key, 21), (SPHERES, NCOEF), jnp.float32, math.log(0.02), math.log(0.1)))
    ramp = 1.0 + 2.0 * jnp.arange(SPHERES, dtype=jnp.float32)[:, None] / max(SPHERES - 1, 1)
    return rate * ramp


def draw_detector(key, part):
    rate = jnp.exp(jax.random.uniform(jax.random.fold_in(key, 31), (POLAR, AZIM), jnp.float32, math.log(0.002), math.log(0.02)))
    ramp = 1.0 + 2.0 * jnp.arange(POLAR, dtype=jnp.float32)[:, None] / max(POLAR - 1, 1)
    return rate * ramp


def touch_ends(values, key, smallest, largest):
    extent = values.shape
    place = [jax.random.randint(jax.random.fold_in(key, axis), (), 0, extent[axis]) for axis in range(len(extent))]
    values = values.at[tuple(place)].set(smallest)
    longest = extent.index(max(extent))
    place[longest] = (place[longest] + 1) % extent[longest]
    return values.at[tuple(place)].set(largest)


def shard_levels(key, shape, pieces, smallest, high):
    def one(axis_at, shards_of):
        draws = jax.random.uniform(jax.random.fold_in(jax.random.fold_in(key, 6), axis_at), (shards_of,), jnp.float32, smallest / len(pieces), high / len(pieces))
        return jnp.repeat(jnp.exp(draws), shape[axis_at] // shards_of).reshape((-1,) + (1,) * (len(shape) - axis_at - 1))

    factor_of = one(*pieces[0])
    for cut in pieces[1:]:
        factor_of = factor_of * one(*cut)
    return factor_of


def bell_draw(rng, dims, scale, bound, shards=(), kind=jnp.bfloat16):
    loudness = shard_levels(rng, dims, shards, -0.22, 0.18) if shards else 1.0
    values = jax.random.normal(rng, dims, jnp.float32) * scale * loudness
    return jnp.minimum(jnp.maximum(values, -bound), bound).astype(kind)


def setup_inputs(seed: int = 0) -> dict:
    key_of = jax.random.split(jax.random.key(seed), 7)
    coefficients = bell_draw(key_of[0], (SPHERES, NCOEF, 2 * FIELDS), 0.005, 0.039794922, ((0, 32),))
    positions = touch_ends(jax.random.randint(key_of[1], (SPHERES, 3), 0, GRID), jax.random.fold_in(key_of[1], 1), 0, GRID - 1).astype(jnp.int32)
    shift_tables = draw_shift_tables(jax.random.fold_in(key_of[6], 71), 0)
    absorb_weight = draw_absorb_weight(jax.random.fold_in(key_of[6], 71), 0)
    incident = bell_draw(key_of[4], (NCOEF, 2 * FIELDS), 0.2, 1.6, (), jnp.float32)
    detector = draw_detector(jax.random.fold_in(key_of[6], 71), 0)
    return dict(coefficients=coefficients, positions=positions, shift_tables=shift_tables, absorb_weight=absorb_weight, incident=incident, detector=detector)


def legendre_table(cos_theta, sine_theta, order):
    values = {}
    values[0, 0] = jnp.zeros_like(cos_theta) + 1.0 / math.sqrt(4.0 * math.pi)
    for azim_order in range(order + 1):
        if azim_order > 0:
            factor = -math.sqrt((2.0 * azim_order + 1.0) / (2.0 * azim_order))
            values[azim_order, azim_order] = factor * sine_theta * values[azim_order - 1, azim_order - 1]
        if azim_order + 1 <= order:
            values[azim_order + 1, azim_order] = math.sqrt(2.0 * azim_order + 3.0) * cos_theta * values[azim_order, azim_order]
        for degree in range(azim_order + 2, order + 1):
            upper_coef = math.sqrt((4.0 * degree * degree - 1.0) / (degree * degree - azim_order * azim_order))
            lower_coef = math.sqrt(((degree - 1.0) * (degree - 1.0) - azim_order * azim_order) / (4.0 * (degree - 1.0) * (degree - 1.0) - 1.0))
            values[degree, azim_order] = upper_coef * (cos_theta * values[degree - 1, azim_order] - lower_coef * values[degree - 2, azim_order])
    return values

def angular_basis(polar_index, azim_index, polar_total, azim_total, order):
    theta = (polar_index.astype(jnp.float32) + 0.5) * (math.pi / polar_total)
    azimuth = azim_index.astype(jnp.float32) * (2.0 * math.pi / azim_total)
    cos_theta = jnp.cos(theta)
    sine_theta = jnp.sin(theta)
    legendre_values = legendre_table(cos_theta, sine_theta, order)
    pi_terms = []
    tau_terms = []
    orders_list = []
    phase_real = []
    phase_imag = []
    unit_powers = [(1.0, 0.0), (0.0, -1.0), (-1.0, 0.0), (0.0, 1.0)]
    for degree in range(1, order + 1):
        norm_factor = 1.0 / math.sqrt(degree * (degree + 1.0))
        power_real, power_imag = unit_powers[(degree + 1) % 4]
        for azim_order in range(-degree, degree + 1):
            size_m = abs(azim_order)
            current = legendre_values[degree, size_m]
            if degree - 1 >= size_m:
                previous = legendre_values[degree - 1, size_m]
            else:
                previous = jnp.zeros_like(current)
            link = math.sqrt((2.0 * degree + 1.0) * (degree * degree - azim_order * azim_order) / (2.0 * degree - 1.0))
            pi_terms.append(azim_order * current / sine_theta)
            tau_terms.append((degree * cos_theta * current - link * previous) / sine_theta)
            orders_list.append(float(azim_order))
            phase_real.append(power_real * norm_factor)
            phase_imag.append(power_imag * norm_factor)
    pi_block = jnp.stack(pi_terms, axis=1)[:, None, :]
    tau_block = jnp.stack(tau_terms, axis=1)[:, None, :]
    orders_row = jnp.array(orders_list, dtype=jnp.float32)
    angle_table = azimuth[:, None] * orders_row[None, :]
    cos_table = jnp.cos(angle_table)
    sin_table = jnp.sin(angle_table)
    scale_real = jnp.array(phase_real, dtype=jnp.float32)[None, :]
    scale_imag = jnp.array(phase_imag, dtype=jnp.float32)[None, :]
    wave_real = (scale_real * cos_table - scale_imag * sin_table)[None, :, :]
    wave_imag = (scale_real * sin_table + scale_imag * cos_table)[None, :, :]
    theta_real = jnp.concatenate([-pi_block * wave_imag, tau_block * wave_real], axis=-1)
    theta_imag = jnp.concatenate([pi_block * wave_real, tau_block * wave_imag], axis=-1)
    phi_real = jnp.concatenate([-tau_block * wave_real, -pi_block * wave_imag], axis=-1)
    phi_imag = jnp.concatenate([-tau_block * wave_imag, pi_block * wave_real], axis=-1)
    real_part = jnp.stack([theta_real, phi_real])
    imag_part = jnp.stack([theta_imag, phi_imag])
    return (real_part, imag_part, sine_theta)

def evaluate_far(real_part, imag_part, anchor):
    half = anchor.shape[1] // 2
    first = jnp.einsum('cikp,pf->cikf', real_part, anchor, precision=lax.Precision.HIGHEST)
    second = jnp.einsum('cikp,pf->cikf', imag_part, anchor, precision=lax.Precision.HIGHEST)
    real_out = first[..., :half] - second[..., half:]
    imag_out = first[..., half:] + second[..., :half]
    return jnp.stack([real_out, imag_out], axis=1)

def rotate_step(matrix, vector):
    product = jnp.einsum('sap,spf->saf', matrix.astype(jnp.float32), vector.astype(jnp.float32))
    half_rows = matrix.shape[2]
    half_cols = vector.shape[2] // 2
    real_out = product[:, :half_rows, :half_cols] - product[:, half_rows:, half_cols:]
    imag_out = product[:, half_rows:, :half_cols] + product[:, :half_rows, half_cols:]
    return jnp.concatenate([real_out, imag_out], axis=2)

def reference(coefficients, positions, shift_tables, absorb_weight, incident, detector):
    blocks = coefficients.shape[0] // SPH_DEV
    coef_blocks = coefficients.reshape(blocks, SPH_DEV, NCOEF, 2 * FIELDS)
    cell_blocks = positions.reshape(blocks, SPH_DEV, 3)
    weight_blocks = absorb_weight.reshape(blocks, SPH_DEV, NCOEF)

    def accumulate(carry, inputs):
        anchor_acc, absorbed_acc = carry
        block_coef, block_cells, block_weight = inputs
        along_z = jnp.take(shift_tables[2], block_cells[:, 2], axis=0)
        along_y = jnp.take(shift_tables[1], block_cells[:, 1], axis=0)
        along_x = jnp.take(shift_tables[0], block_cells[:, 0], axis=0)
        first = rotate_step(along_z, block_coef).astype(jnp.bfloat16)
        second = rotate_step(along_y, first).astype(jnp.bfloat16)
        moved = rotate_step(along_x, second)
        widened = block_coef.astype(jnp.float32)
        squares = widened * widened
        energy = squares[:, :, :FIELDS] + squares[:, :, FIELDS:]
        absorbed_acc = absorbed_acc + jnp.einsum('sp,spf->f', block_weight, energy)
        return ((anchor_acc + lax.optimization_barrier(jnp.sum(moved, axis=0)), absorbed_acc), None)
    start = (jnp.zeros((NCOEF, 2 * FIELDS), jnp.float32), jnp.zeros((FIELDS,), jnp.float32))
    (anchor, absorbed), ignored = lax.scan(accumulate, start, (coef_blocks, cell_blocks, weight_blocks))
    extinction = lax.optimization_barrier(jnp.sum(incident[:, :FIELDS] * anchor[:, :FIELDS] + incident[:, FIELDS:] * anchor[:, FIELDS:], axis=0))
    real_part, imag_part, sine_theta = angular_basis(jnp.arange(POLAR), jnp.arange(AZIM), POLAR, AZIM, ORDER)
    amplitude = evaluate_far(real_part, imag_part, anchor)
    weight = detector * sine_theta[:, None] * (2.0 * math.pi * math.pi / (POLAR * AZIM))
    collected = jnp.einsum('crikf,ik->f', amplitude * amplitude, weight)
    cross_sections = jnp.stack([extinction, absorbed, collected])
    return (amplitude, cross_sections)
```

```python
import functools
import math

import jax
import jax.numpy as jnp
import numpy as np
from jax import lax
from jax.experimental import pallas as pl
from jax.experimental.pallas import tpu as pltpu
from jax.sharding import PartitionSpec as P

MESH = pl.DeviceIdType.MESH


def angular_tables(polar_total, azim_total, order):
    theta = (np.arange(polar_total) + 0.5) * (math.pi / polar_total)
    azimuth = np.arange(azim_total) * (2.0 * math.pi / azim_total)
    cos_theta, sine = np.cos(theta), np.sin(theta)
    leg = {(0, 0): np.full_like(theta, 1.0 / math.sqrt(4.0 * math.pi))}
    for m in range(order + 1):
        if m > 0:
            leg[m, m] = -math.sqrt((2.0 * m + 1.0) / (2.0 * m)) * sine * leg[m - 1, m - 1]
        if m + 1 <= order:
            leg[m + 1, m] = math.sqrt(2.0 * m + 3.0) * cos_theta * leg[m, m]
        for n in range(m + 2, order + 1):
            upper = math.sqrt((4.0 * n * n - 1.0) / (n * n - m * m))
            lower = math.sqrt(((n - 1.0) ** 2 - m * m) / (4.0 * (n - 1.0) ** 2 - 1.0))
            leg[n, m] = upper * (cos_theta * leg[n - 1, m] - lower * leg[n - 2, m])
    pis, taus, waves = [], [], []
    for n in range(1, order + 1):
        for m in range(-n, n + 1):
            s = abs(m)
            prev = leg[n - 1, s] if n - 1 >= s else np.zeros_like(theta)
            link = math.sqrt((2.0 * n + 1.0) * (n * n - m * m) / (2.0 * n - 1.0))
            pis.append(m * leg[n, s] / sine)
            taus.append((n * cos_theta * leg[n, s] - link * prev) / sine)
            unit = (1.0, -1j, -1.0, 1j)[(n + 1) % 4]
            waves.append(unit * np.exp(1j * m * azimuth) / math.sqrt(n * (n + 1.0)))
    pi, tau, wave = np.stack(pis, 1), np.stack(taus, 1), np.stack(waves, 1)
    wr, wi = wave.real, wave.imag
    polar = np.stack([np.concatenate([pi, tau] * 2, 1), np.concatenate([tau, pi] * 2, 1)])
    azim = np.stack([
        np.concatenate([-wi, wr, -wr, -wi], 1),
        np.concatenate([wr, wi, -wi, wr], 1),
        np.concatenate([-wr, -wi, wi, -wr], 1),
        np.concatenate([-wi, wr, -wr, -wi], 1),
    ])
    return polar, azim, sine


def rotate(table, real, imag):
    half = table.shape[0] // 2
    width = real.shape[1]
    product = jnp.dot(table, jnp.concatenate([real, imag], 1), preferred_element_type=jnp.float32)
    return (
        product[:half, :width] - product[half:, width:],
        product[half:, :width] + product[:half, width:],
    )


def local_kernel(chunks, pos_ref, c_ref, z_ref, y_ref, x_ref, aw_ref, out_ref):
    j = pl.program_id(0)
    coef = c_ref.shape[1]
    fields = c_ref.shape[2] // 2
    width = fields // chunks

    @pl.when(j == 0)
    def _():
        out_ref[...] = jnp.zeros_like(out_ref)

    lane = lax.broadcasted_iota(jnp.int32, aw_ref.shape, 1)
    column = jnp.sum(jnp.where(lane == j, aw_ref[...], 0.0), axis=1, keepdims=True)
    for h in range(chunks):
        cols = slice(h * width, (h + 1) * width)
        vr = c_ref[0, :, cols]
        vi = c_ref[0, :, slice(fields + h * width, fields + (h + 1) * width)]
        fr, fi = rotate(z_ref[0, 0], vr, vi)
        fr, fi = rotate(y_ref[0, 0], fr.astype(jnp.bfloat16), fi.astype(jnp.bfloat16))
        fr, fi = rotate(x_ref[0, 0], fr.astype(jnp.bfloat16), fi.astype(jnp.bfloat16))
        out_ref[:coef, cols] += fr
        out_ref[coef : 2 * coef, cols] += fi
        wr, wi = vr.astype(jnp.float32), vi.astype(jnp.float32)
        energy = (wr * wr + wi * wi) * column
        out_ref[2 * coef : 2 * coef + 1, cols] += jnp.sum(energy, axis=0, keepdims=True)


def local_part(coefficients, positions, shift_tables, absorb_weight, rows):
    spheres, coef, columns = coefficients.shape
    fields = columns // 2

    def table(axis):
        return pl.BlockSpec((1, 1, 2 * coef, coef), lambda j, pos: (axis, pos[j, axis], 0, 0))

    return pl.pallas_call(
        functools.partial(local_kernel, 2),
        grid_spec=pltpu.PrefetchScalarGridSpec(
            num_scalar_prefetch=1,
            grid=(spheres,),
            in_specs=[
                pl.BlockSpec((1, coef, columns), lambda j, pos: (j, 0, 0)),
                table(2),
                table(1),
                table(0),
                pl.BlockSpec((coef, spheres), lambda j, pos: (0, 0)),
            ],
            out_specs=pl.BlockSpec((rows, fields), lambda j, pos: (0, 0)),
        ),
        out_shape=jax.ShapeDtypeStruct((rows, fields), jnp.float32),
        compiler_params=pltpu.CompilerParams(dimension_semantics=("arbitrary",)),
    )(positions, coefficients, shift_tables, shift_tables, shift_tables, absorb_weight.T)


def split(value):
    high = value.astype(jnp.bfloat16)
    return high, (value - high.astype(jnp.float32)).astype(jnp.bfloat16)


def far_kernel(
    sph_n, ang_n, coef, pol,
    part, det, inc_hbm, pol_hbm, azi_hbm, amp_hbm, stats,
    h_in, acc, recv1, gath, inc, tpol, tazi, basis, amp, pow_send, pow_recv,
    s0, r0, s1, r1, s2, r2, s3, r3, s4, r4, lsem,
):
    n = sph_n * ang_n
    pairs = ang_n // 2
    m = n // 2
    sph, ang = lax.axis_index("sph"), lax.axis_index("ang")
    p = lax.rem(ang, 2)
    chip = sph * pairs + ang // 2
    me = sph * ang_n + ang
    partner = (sph, ang + 1 - 2 * p)

    def peer(c):
        return (c // pairs, 2 * lax.rem(c, pairs) + p)

    def device(d):
        return (d // ang_n, lax.rem(d, ang_n))

    local = [
        pltpu.make_async_copy(inc_hbm, inc, lsem.at[0]),
        pltpu.make_async_copy(pol_hbm.at[sph], tpol, lsem.at[1]),
        pltpu.make_async_copy(azi_hbm.at[ang], tazi, lsem.at[2]),
    ]
    for copy in local:
        copy.start()

    barrier = pltpu.get_barrier_semaphore()

    def greet(k, carry):
        pl.semaphore_signal(
            barrier, inc=1, device_id=device(lax.rem(me + k, n)), device_id_type=MESH
        )
        return carry

    lax.fori_loop(1, n, greet, 0)
    pl.semaphore_wait(barrier, n - 1)

    def copy0(c):
        return pltpu.make_async_remote_copy(
            part.at[(1 - p) * m + c], h_in.at[c], s0.at[c], r0.at[c], partner, MESH
        )

    def copy1(c, slot):
        return pltpu.make_async_remote_copy(
            acc.at[c], recv1.at[slot], s1.at[c], r1.at[slot], peer(c), MESH
        )

    def copy2(c, slot):
        row = gath.at[p * m + slot]
        return pltpu.make_async_remote_copy(row, row, s2.at[c], r2.at[slot], peer(c), MESH)

    def copy3(c, half):
        row = gath.at[half * m + c]
        return pltpu.make_async_remote_copy(row, row, s3.at[c], r3.at[c], partner, MESH)

    def copy4(d, slot):
        return pltpu.make_async_remote_copy(
            pow_send, pow_recv.at[slot], s4.at[d], r4.at[slot], device(d), MESH
        )

    def loop(low, high, body):
        def step(k, carry):
            body(k)
            return carry

        lax.fori_loop(low, high, step, 0)

    loop(1, m + 1, lambda k: copy0(lax.rem(chip + k, m)).start())

    def first(c):
        copy0(c).wait_recv()
        acc[c] = part[p * m + c] + h_in[c]

    def exchange(k):
        c = lax.rem(chip + k, m)
        first(c)
        copy1(c, chip).start()

    loop(1, m, exchange)
    first(chip)

    for copy in local:
        copy.wait()
    azi = tazi.shape[1]
    block = pol * azi
    for cr in range(4):
        for i in range(pol):
            basis[cr * block + i * azi : cr * block + (i + 1) * azi, :] = (
                tpol[cr // 2, i : i + 1, :] * tazi[cr]
            )

    def gather_sum(k, total):
        c = lax.rem(chip - k + m, m)
        copy1(c, c).wait_recv()
        return total + recv1[c]

    gath[p * m + chip] = lax.fori_loop(1, m, gather_sum, acc[chip])
    copy3(chip, p).start()
    loop(1, m, lambda k: copy2(lax.rem(chip + k, m), chip).start())

    def forward(k):
        c = lax.rem(chip - k + m, m)
        copy2(c, c).wait_recv()
        copy3(c, p).start()

    loop(1, m, forward)
    loop(0, m, lambda k: copy3(k, 1 - p).wait_recv())

    rows = gath.shape[0] * gath.shape[1]
    fields = gath.shape[2]
    anchor = gath[...].reshape(rows, fields)
    a_high, a_low = split(anchor[: 2 * coef])
    w_high, w_low = split(basis[:, : 2 * coef])
    dot = functools.partial(jnp.dot, preferred_element_type=jnp.float32)
    far = dot(w_high, a_high) + (dot(w_high, a_low) + dot(w_low, a_high))
    amp[...] = far
    out_copy = pltpu.make_async_copy(amp, amp_hbm, lsem.at[0])
    out_copy.start()

    azim_total = det.shape[1]
    want = lax.broadcasted_iota(jnp.int32, (azi, azim_total), 0) + ang * azi
    lane = lax.broadcasted_iota(jnp.int32, (azi, azim_total), 1)
    power = jnp.zeros((1, fields), jnp.float32)
    for i in range(pol):
        weight = jnp.sum(
            jnp.where(lane == want, det[i : i + 1, :], 0.0), axis=1, keepdims=True
        ) * tpol[0, i : i + 1, 2 * coef : 2 * coef + 1]
        total = jnp.zeros((azi, fields), jnp.float32)
        for cr in range(4):
            piece = far[cr * block + i * azi : cr * block + (i + 1) * azi, :]
            total = total + piece * piece
        power = power + jnp.sum(total * weight, axis=0, keepdims=True)
    pow_send[...] = power
    pow_recv[me] = power
    loop(1, n, lambda k: copy4(lax.rem(me + k, n), me).start())

    stats[0:1, :] = jnp.sum(
        inc[:, :fields] * anchor[:coef] + inc[:, fields:] * anchor[coef : 2 * coef],
        axis=0, keepdims=True,
    )
    stats[1:2, :] = anchor[2 * coef : 2 * coef + 1]

    def finish(k):
        copy0(k).wait_send()
        copy3(k, p).wait_send()

    loop(0, m, finish)

    def finish_peers(k):
        c = lax.rem(chip + k, m)
        copy1(c, chip).wait_send()
        copy2(c, chip).wait_send()

    loop(1, m, finish_peers)

    def finish_power(k):
        d = lax.rem(me + k, n)
        copy4(d, d).wait_recv()
        copy4(d, me).wait_send()

    loop(1, n, finish_power)
    stats[2:3, :] = lax.fori_loop(
        1, n, lambda k, total: total + pow_recv[k], pow_recv[0]
    )
    out_copy.wait()


def far_part(part, detector, incident, polar, azim, sph_n, ang_n):
    n, r, fields = part.shape
    m = n // 2
    coef = incident.shape[0]
    pol = detector.shape[0]
    azi = azim.shape[2]
    wide = polar.shape[3]
    vmem = pl.BlockSpec(memory_space=pltpu.VMEM)
    hbm = pl.BlockSpec(memory_space=pl.ANY)
    f32 = jnp.float32
    dma = pltpu.SemaphoreType.DMA
    return pl.pallas_call(
        functools.partial(far_kernel, sph_n, ang_n, coef, pol),
        out_shape=(
            jax.ShapeDtypeStruct((4 * pol * azi, fields), f32),
            jax.ShapeDtypeStruct((3, fields), f32),
        ),
        in_specs=[vmem, vmem, hbm, hbm, hbm],
        out_specs=(hbm, vmem),
        scratch_shapes=[
            pltpu.VMEM((m, r, fields), f32),
            pltpu.VMEM((m, r, fields), f32),
            pltpu.VMEM((m, r, fields), f32),
            pltpu.VMEM((n, r, fields), f32),
            pltpu.VMEM(incident.shape, f32),
            pltpu.VMEM((2, pol, wide), f32),
            pltpu.VMEM((4, azi, wide), f32),
            pltpu.VMEM((4 * pol * azi, wide), f32),
            pltpu.VMEM((4 * pol * azi, fields), f32),
            pltpu.VMEM((1, fields), f32),
            pltpu.VMEM((n, 1, fields), f32),
        ]
        + [dma((m,))] * 8
        + [dma((n,))] * 2
        + [dma((3,))],
        compiler_params=pltpu.CompilerParams(
            collective_id=0, has_side_effects=True, vmem_limit_bytes=48 * 2**20
        ),
    )(part, detector, incident, polar, azim)


def shards(sph_n, ang_n, coefficients, positions, shift_tables, absorb_weight, incident, detector):
    fields = coefficients.shape[2] // 2
    coef = coefficients.shape[1]
    n = sph_n * ang_n
    chunk = 8 * -(-(2 * coef + 1) // (8 * n))
    pol, azim_total = detector.shape
    polar_total = pol * sph_n
    azi = azim_total // ang_n
    order = math.isqrt(coef // 2 + 1) - 1
    wide = 128 * -(-(2 * coef + 1) // 128)
    polar, azim, sine = angular_tables(polar_total, azim_total, order)
    table_polar = np.zeros((sph_n, 2, pol, wide), np.float32)
    table_polar[..., : 2 * coef] = polar.reshape(2, sph_n, pol, 2 * coef).transpose(1, 0, 2, 3)
    solid = 2.0 * math.pi * math.pi / (polar_total * azim_total)
    table_polar[..., 2 * coef] = (sine * solid).reshape(sph_n, 1, pol)
    table_azim = np.zeros((ang_n, 4, azi, wide), np.float32)
    table_azim[..., : 2 * coef] = azim.reshape(4, ang_n, azi, 2 * coef).transpose(1, 0, 2, 3)

    part = local_part(coefficients, positions, shift_tables, absorb_weight, n * chunk)
    amplitude, stats = far_part(
        part.reshape(n, chunk, fields), detector, incident,
        jnp.asarray(table_polar), jnp.asarray(table_azim), sph_n, ang_n,
    )
    share = fields // ang_n
    own = lax.dynamic_slice_in_dim(stats, lax.axis_index("ang") * share, share, 1)
    return (amplitude.reshape(2, 2, pol, azi, fields), own)


def solution(mesh):
    placed = (
        P(("sph", "ang"), None, None),
        P(("sph", "ang"), None),
        P(),
        P(("sph", "ang"), None),
        P(),
        P("sph", None),
    )
    return jax.shard_map(
        functools.partial(shards, mesh.shape["sph"], mesh.shape["ang"]),
        mesh=mesh,
        in_specs=placed,
        out_specs=(P(None, None, "sph", "ang", None), P(None, "ang")),
        check_vma=False,
    )
```

```python
import functools
import math

import jax
import jax.numpy as jnp
import numpy as np
from jax import lax
from jax.experimental import pallas as pl
from jax.experimental.pallas import tpu as pltpu
from jax.sharding import PartitionSpec as P

MESH = pl.DeviceIdType.MESH


def angular_tables(polar_total, azim_total, order):
    theta = (np.arange(polar_total) + 0.5) * (math.pi / polar_total)
    azimuth = np.arange(azim_total) * (2.0 * math.pi / azim_total)
    cos_theta, sine = np.cos(theta), np.sin(theta)
    leg = {(0, 0): np.full_like(theta, 1.0 / math.sqrt(4.0 * math.pi))}
    for m in range(order + 1):
        if m > 0:
            leg[m, m] = -math.sqrt((2.0 * m + 1.0) / (2.0 * m)) * sine * leg[m - 1, m - 1]
        if m + 1 <= order:
            leg[m + 1, m] = math.sqrt(2.0 * m + 3.0) * cos_theta * leg[m, m]
        for n in range(m + 2, order + 1):
            upper = math.sqrt((4.0 * n * n - 1.0) / (n * n - m * m))
            lower = math.sqrt(((n - 1.0) ** 2 - m * m) / (4.0 * (n - 1.0) ** 2 - 1.0))
            leg[n, m] = upper * (cos_theta * leg[n - 1, m] - lower * leg[n - 2, m])
    pis, taus, waves = [], [], []
    for n in range(1, order + 1):
        for m in range(-n, n + 1):
            s = abs(m)
            prev = leg[n - 1, s] if n - 1 >= s else np.zeros_like(theta)
            link = math.sqrt((2.0 * n + 1.0) * (n * n - m * m) / (2.0 * n - 1.0))
            pis.append(m * leg[n, s] / sine)
            taus.append((n * cos_theta * leg[n, s] - link * prev) / sine)
            unit = (1.0, -1j, -1.0, 1j)[(n + 1) % 4]
            waves.append(unit * np.exp(1j * m * azimuth) / math.sqrt(n * (n + 1.0)))
    pi, tau, wave = np.stack(pis, 1), np.stack(taus, 1), np.stack(waves, 1)
    wr, wi = wave.real, wave.imag
    polar = np.stack([np.concatenate([pi, tau] * 2, 1), np.concatenate([tau, pi] * 2, 1)])
    azim = np.stack([
        np.concatenate([-wi, wr, -wr, -wi], 1),
        np.concatenate([wr, wi, -wi, wr], 1),
        np.concatenate([-wr, -wi, wi, -wr], 1),
        np.concatenate([-wi, wr, -wr, -wi], 1),
    ])
    return polar, azim, sine


def rotate(table, real, imag):
    half = table.shape[0] // 2
    width = real.shape[1]
    product = jnp.dot(table, jnp.concatenate([real, imag], 1), preferred_element_type=jnp.float32)
    return (
        product[:half, :width] - product[half:, width:],
        product[half:, :width] + product[:half, width:],
    )


def local_kernel(chunks, pos_ref, c_ref, z_ref, y_ref, x_ref, aw_ref, out_ref):
    j = pl.program_id(0)
    coef = c_ref.shape[1]
    fields = c_ref.shape[2] // 2
    width = fields // chunks

    @pl.when(j == 0)
    def _():
        out_ref[...] = jnp.zeros_like(out_ref)

    weight = aw_ref[...].T
    lane = lax.broadcasted_iota(jnp.int32, weight.shape, 1)
    column = jnp.sum(jnp.where(lane == j, weight, 0.0), axis=1, keepdims=True)
    for h in range(chunks):
        cols = slice(h * width, (h + 1) * width)
        vr = c_ref[0, :, cols]
        vi = c_ref[0, :, slice(fields + h * width, fields + (h + 1) * width)]
        fr, fi = rotate(z_ref[0, 0], vr, vi)
        fr, fi = rotate(y_ref[0, 0], fr.astype(jnp.bfloat16), fi.astype(jnp.bfloat16))
        fr, fi = rotate(x_ref[0, 0], fr.astype(jnp.bfloat16), fi.astype(jnp.bfloat16))
        out_ref[:coef, cols] += fr
        out_ref[coef : 2 * coef, cols] += fi
        wr, wi = vr.astype(jnp.float32), vi.astype(jnp.float32)
        energy = (wr * wr + wi * wi) * column
        out_ref[2 * coef : 2 * coef + 1, cols] += jnp.sum(energy, axis=0, keepdims=True)


def local_part(coefficients, positions, shift_tables, absorb_weight, rows):
    spheres, coef, columns = coefficients.shape
    fields = columns // 2

    def table(axis):
        return pl.BlockSpec((1, 1, 2 * coef, coef), lambda j, pos: (axis, pos[axis, j], 0, 0))

    return pl.pallas_call(
        functools.partial(local_kernel, 1),
        grid_spec=pltpu.PrefetchScalarGridSpec(
            num_scalar_prefetch=1,
            grid=(spheres,),
            in_specs=[
                pl.BlockSpec((1, coef, columns), lambda j, pos: (j, 0, 0)),
                table(2),
                table(1),
                table(0),
                pl.BlockSpec((spheres, coef), lambda j, pos: (0, 0)),
            ],
            out_specs=pl.BlockSpec(memory_space=pltpu.VMEM),
        ),
        out_shape=jax.ShapeDtypeStruct((rows, fields), jnp.float32),
        compiler_params=pltpu.CompilerParams(dimension_semantics=("arbitrary",)),
    )(positions.T, coefficients, shift_tables, shift_tables, shift_tables, absorb_weight)


def split(value):
    high = value.astype(jnp.bfloat16)
    return high, (value - high.astype(jnp.float32)).astype(jnp.bfloat16)


def far_kernel(
    sph_n, ang_n, coef, pol,
    part, det, inc_hbm, pol_hbm, azi_hbm, amp_hbm, stats,
    h_in, acc, in_a, in_b, in_z, gath, inc, tpol, tazi, basis, amp, pow_send, pow_recv,
    s0, r0, sa, ra, sb, rb, sz, rz, ga, gb, gz, rg, s3, r3, s4, r4, lsem,
):
    n = sph_n * ang_n
    q = ang_n // 2
    nz = sph_n // q
    m = n // 2
    sph, ang = lax.axis_index("sph"), lax.axis_index("ang")
    p = lax.rem(ang, 2)
    x, y, z = lax.rem(sph, q), ang // 2, sph // q
    a = x * (1 - p) + y * p
    b = y * (1 - p) + x * p
    chip = (a * q + b) * nz + z
    me = sph * ang_n + ang
    partner = (sph, ang + 1 - 2 * p)

    def peer(a2, b2, z2):
        x2 = a2 * (1 - p) + b2 * p
        y2 = b2 * (1 - p) + a2 * p
        return (z2 * q + x2, 2 * y2 + p)

    def at(a2, b2, z2):
        return (a2 * q + b2) * nz + z2

    def device(d):
        return (d // ang_n, lax.rem(d, ang_n))

    local = [
        pltpu.make_async_copy(inc_hbm, inc, lsem.at[0]),
        pltpu.make_async_copy(pol_hbm.at[sph], tpol, lsem.at[1]),
        pltpu.make_async_copy(azi_hbm.at[ang], tazi, lsem.at[2]),
    ]
    for copy in local:
        copy.start()

    barrier = pltpu.get_barrier_semaphore()

    def greet(k, carry):
        pl.semaphore_signal(
            barrier, inc=1, device_id=device(lax.rem(me + k, n)), device_id_type=MESH
        )
        return carry

    lax.fori_loop(1, n, greet, 0)
    pl.semaphore_wait(barrier, n - 1)

    remote = pltpu.make_async_remote_copy

    def copy0(c):
        return remote(part.at[(1 - p) * m + c], h_in.at[c], s0.at[c], r0.at[c], partner, MESH)

    def send_a(a2, i, src):
        return remote(
            acc.at[a2 * q * nz + i], in_a.at[src * q * nz + i],
            sa.at[a2 * q * nz + i], ra.at[src * q * nz + i], peer(a2, b, z), MESH,
        )

    def send_b(b2, z2, src):
        return remote(
            acc.at[at(a, b2, z2)], in_b.at[src * nz + z2],
            sb.at[b2 * nz + z2], rb.at[src * nz + z2], peer(a, b2, z), MESH,
        )

    def send_z(z2, src):
        return remote(
            acc.at[at(a, b, z2)], in_z.at[src], sz.at[z2], rz.at[src], peer(a, b, z2), MESH
        )

    def spread(c, send, device_id):
        row = gath.at[p * m + c]
        return remote(row, row, send, rg.at[c], device_id, MESH)

    def spread_a(a2, b2, z2):
        return spread(at(a, b2, z2), ga.at[at(a2, b2, z2)], peer(a2, b, z))

    def spread_b(b2, z2):
        return spread(at(a, b, z2), gb.at[b2 * nz + z2], peer(a, b2, z))

    def spread_z(z2):
        return spread(chip, gz.at[z2], peer(a, b, z2))

    def arrived(c):
        spread(c, gz.at[0], partner).wait_recv()

    def copy3(c, half):
        row = gath.at[half * m + c]
        return remote(row, row, s3.at[c], r3.at[c], partner, MESH)

    def copy4(d, slot):
        return pltpu.make_async_remote_copy(
            pow_send, pow_recv.at[slot], s4.at[d], r4.at[slot], device(d), MESH
        )

    def loop(low, high, body):
        def step(k, carry):
            body(k)
            return carry

        lax.fori_loop(low, high, step, 0)

    def shift(base, k, size):
        return lax.rem(base + k, size)

    loop(1, m + 1, lambda k: copy0(shift(b * q * nz + q * nz - 1, k, m)).start())

    def first(c):
        copy0(c).wait_recv()
        acc[c] = part[p * m + c] + h_in[c]

    for da in range(1, q):
        a2 = shift(a, da, q)

        def step_a(k):
            i = shift((b + 1) * nz, k, q * nz)
            first(a2 * q * nz + i)
            send_a(a2, i, a).start()

        loop(0, q * nz, step_a)

    def add_a(b2, z2):
        c = at(a, b2, z2)
        first(c)
        value = acc[c]
        for da in range(1, q):
            src = shift(a, da, q)
            send_a(src, b2 * nz + z2, src).wait_recv()
            value = value + in_a[at(src, b2, z2)]
        acc[c] = value

    for db in range(1, q):
        b2 = shift(b, db, q)

        def step_b(k):
            z2 = shift(z, k, nz)
            add_a(b2, z2)
            send_b(b2, z2, b).start()

        loop(1, nz + 1, step_b)

    def add_b(z2):
        add_a(b, z2)
        value = acc[at(a, b, z2)]
        for db in range(1, q):
            src = shift(b, db, q)
            send_b(src, z2, src).wait_recv()
            value = value + in_b[src * nz + z2]
        acc[at(a, b, z2)] = value

    def step_z(k):
        z2 = shift(z, k, nz)
        add_b(z2)
        send_z(z2, z).start()

    loop(1, nz, step_z)
    add_b(z)

    for copy in local:
        copy.wait()
    azi = tazi.shape[1]
    block = pol * azi
    for cr in range(4):
        for i in range(pol):
            basis[cr * block + i * azi : cr * block + (i + 1) * azi, :] = (
                tpol[cr // 2, i : i + 1, :] * tazi[cr]
            )

    def gather_sum(k, total):
        src = shift(z, k, nz)
        send_z(src, src).wait_recv()
        return total + in_z[src]

    gath[p * m + chip] = lax.fori_loop(1, nz, gather_sum, acc[chip])
    loop(1, nz, lambda k: spread_z(shift(z, k, nz)).start())

    def plane(k):
        z2 = shift(z, k, nz)
        if_own = at(a, b, z2)
        for db in range(1, q):
            spread_b(shift(b, db, q), z2).start()
        for da in range(1, q):
            spread_a(shift(a, da, q), b, z2).start()
        copy3(if_own, p).start()

    plane(0)

    def step_plane(k):
        arrived(at(a, b, shift(z, k, nz)))
        plane(k)

    loop(1, nz, step_plane)

    def step_line(k):
        z2 = shift(z, k, nz)
        for db in range(1, q):
            b2 = shift(b, db, q)
            arrived(at(a, b2, z2))
            for da in range(1, q):
                spread_a(shift(a, da, q), b2, z2).start()
            copy3(at(a, b2, z2), p).start()

    loop(0, nz, step_line)

    def step_rest(k):
        for db in range(q):
            for da in range(1, q):
                c = at(shift(a, da, q), shift(b, db, q), shift(z, k, nz))
                arrived(c)
                copy3(c, p).start()

    loop(0, nz, step_rest)
    loop(0, m, lambda k: copy3(k, 1 - p).wait_recv())

    rows = gath.shape[0] * gath.shape[1]
    fields = gath.shape[2]
    anchor = gath[...].reshape(rows, fields)
    a_high, a_low = split(anchor[: 2 * coef])
    w_high, w_low = split(basis[:, : 2 * coef])
    dot = functools.partial(jnp.dot, preferred_element_type=jnp.float32)
    far = dot(w_high, a_high) + (dot(w_high, a_low) + dot(w_low, a_high))
    amp[...] = far
    out_copy = pltpu.make_async_copy(amp, amp_hbm, lsem.at[0])
    out_copy.start()

    azim_total = det.shape[1]
    want = lax.broadcasted_iota(jnp.int32, (azi, azim_total), 0) + ang * azi
    lane = lax.broadcasted_iota(jnp.int32, (azi, azim_total), 1)
    power = jnp.zeros((1, fields), jnp.float32)
    for i in range(pol):
        weight = jnp.sum(
            jnp.where(lane == want, det[i : i + 1, :], 0.0), axis=1, keepdims=True
        ) * tpol[0, i : i + 1, 2 * coef : 2 * coef + 1]
        total = jnp.zeros((azi, fields), jnp.float32)
        for cr in range(4):
            piece = far[cr * block + i * azi : cr * block + (i + 1) * azi, :]
            total = total + piece * piece
        power = power + jnp.sum(total * weight, axis=0, keepdims=True)
    pow_send[...] = power
    pow_recv[me] = power
    loop(1, n, lambda k: copy4(lax.rem(me + k, n), me).start())

    stats[0:1, :] = jnp.sum(
        inc[:, :fields] * anchor[:coef] + inc[:, fields:] * anchor[coef : 2 * coef],
        axis=0, keepdims=True,
    )
    stats[1:2, :] = anchor[2 * coef : 2 * coef + 1]

    def finish(k):
        copy0(k).wait_send()
        copy3(k, p).wait_send()

    loop(0, m, finish)

    def finish_plane(k):
        for db in range(q):
            b2 = shift(b, db, q)
            for da in range(1, q):
                a2 = shift(a, da, q)
                send_a(a2, b2 * nz + k, a).wait_send()
                spread_a(a2, b2, k).wait_send()
            if db > 0:
                send_b(b2, k, b).wait_send()
                spread_b(b2, k).wait_send()

    loop(0, nz, finish_plane)

    def finish_line(k):
        z2 = shift(z, k, nz)
        send_z(z2, z).wait_send()
        spread_z(z2).wait_send()

    loop(1, nz, finish_line)

    def finish_power(k):
        d = lax.rem(me + k, n)
        copy4(d, d).wait_recv()
        copy4(d, me).wait_send()

    loop(1, n, finish_power)
    stats[2:3, :] = lax.fori_loop(
        1, n, lambda k, total: total + pow_recv[k], pow_recv[0]
    )
    out_copy.wait()


def far_part(part, detector, incident, polar, azim, sph_n, ang_n):
    n, r, fields = part.shape
    m = n // 2
    nz = sph_n // (ang_n // 2)
    line = n // ang_n
    coef = incident.shape[0]
    pol = detector.shape[0]
    azi = azim.shape[2]
    wide = polar.shape[3]
    vmem = pl.BlockSpec(memory_space=pltpu.VMEM)
    hbm = pl.BlockSpec(memory_space=pl.ANY)
    f32 = jnp.float32
    dma = pltpu.SemaphoreType.DMA
    return pl.pallas_call(
        functools.partial(far_kernel, sph_n, ang_n, coef, pol),
        out_shape=(
            jax.ShapeDtypeStruct((4 * pol * azi, fields), f32),
            jax.ShapeDtypeStruct((3, fields), f32),
        ),
        in_specs=[vmem, vmem, hbm, hbm, hbm],
        out_specs=(hbm, vmem),
        scratch_shapes=[
            pltpu.VMEM((m, r, fields), f32),
            pltpu.VMEM((m, r, fields), f32),
            pltpu.VMEM((m, r, fields), f32),
            pltpu.VMEM((line, r, fields), f32),
            pltpu.VMEM((nz, r, fields), f32),
            pltpu.VMEM((n, r, fields), f32),
            pltpu.VMEM(incident.shape, f32),
            pltpu.VMEM((2, pol, wide), f32),
            pltpu.VMEM((4, azi, wide), f32),
            pltpu.VMEM((4 * pol * azi, wide), f32),
            pltpu.VMEM((4 * pol * azi, fields), f32),
            pltpu.VMEM((1, fields), f32),
            pltpu.VMEM((n, 1, fields), f32),
        ]
        + [dma((size,)) for size in (m, m, m, m, line, line, nz, nz, m, line, nz, m, m, m)]
        + [dma((n,))] * 2
        + [dma((3,))],
        compiler_params=pltpu.CompilerParams(
            collective_id=0, has_side_effects=True, vmem_limit_bytes=48 * 2**20
        ),
    )(part, detector, incident, polar, azim)


def shards(sph_n, ang_n, coefficients, positions, shift_tables, absorb_weight, incident, detector):
    fields = coefficients.shape[2] // 2
    coef = coefficients.shape[1]
    n = sph_n * ang_n
    chunk = 8 * -(-(2 * coef + 1) // (8 * n))
    pol, azim_total = detector.shape
    polar_total = pol * sph_n
    azi = azim_total // ang_n
    order = math.isqrt(coef // 2 + 1) - 1
    wide = 128 * -(-(2 * coef + 1) // 128)
    polar, azim, sine = angular_tables(polar_total, azim_total, order)
    table_polar = np.zeros((sph_n, 2, pol, wide), np.float32)
    table_polar[..., : 2 * coef] = polar.reshape(2, sph_n, pol, 2 * coef).transpose(1, 0, 2, 3)
    solid = 2.0 * math.pi * math.pi / (polar_total * azim_total)
    table_polar[..., 2 * coef] = (sine * solid).reshape(sph_n, 1, pol)
    table_azim = np.zeros((ang_n, 4, azi, wide), np.float32)
    table_azim[..., : 2 * coef] = azim.reshape(4, ang_n, azi, 2 * coef).transpose(1, 0, 2, 3)

    part = local_part(coefficients, positions, shift_tables, absorb_weight, n * chunk)
    amplitude, stats = far_part(
        part.reshape(n, chunk, fields), detector, incident,
        jnp.asarray(table_polar), jnp.asarray(table_azim), sph_n, ang_n,
    )
    share = fields // ang_n
    own = lax.dynamic_slice_in_dim(stats, lax.axis_index("ang") * share, share, 1)
    return (amplitude.reshape(2, 2, pol, azi, fields), own)


def solution(mesh):
    placed = (
        P(("sph", "ang"), None, None),
        P(("sph", "ang"), None),
        P(),
        P(("sph", "ang"), None),
        P(),
        P("sph", None),
    )
    return jax.shard_map(
        functools.partial(shards, mesh.shape["sph"], mesh.shape["ang"]),
        mesh=mesh,
        in_specs=placed,
        out_specs=(P(None, None, "sph", "ang", None), P(None, "ang")),
        check_vma=False,
    )
```

```python
import functools
import math

import jax
import jax.numpy as jnp
import numpy as np
from jax import lax
from jax.experimental import pallas as pl
from jax.experimental.pallas import tpu as pltpu
from jax.sharding import PartitionSpec as P

MESH = pl.DeviceIdType.MESH


def angular_tables(polar_total, azim_total, order):
    theta = (np.arange(polar_total) + 0.5) * (math.pi / polar_total)
    azimuth = np.arange(azim_total) * (2.0 * math.pi / azim_total)
    cos_theta, sine = np.cos(theta), np.sin(theta)
    leg = {(0, 0): np.full_like(theta, 1.0 / math.sqrt(4.0 * math.pi))}
    for m in range(order + 1):
        if m > 0:
            leg[m, m] = -math.sqrt((2.0 * m + 1.0) / (2.0 * m)) * sine * leg[m - 1, m - 1]
        if m + 1 <= order:
            leg[m + 1, m] = math.sqrt(2.0 * m + 3.0) * cos_theta * leg[m, m]
        for n in range(m + 2, order + 1):
            upper = math.sqrt((4.0 * n * n - 1.0) / (n * n - m * m))
            lower = math.sqrt(((n - 1.0) ** 2 - m * m) / (4.0 * (n - 1.0) ** 2 - 1.0))
            leg[n, m] = upper * (cos_theta * leg[n - 1, m] - lower * leg[n - 2, m])
    pis, taus, waves = [], [], []
    for n in range(1, order + 1):
        for m in range(-n, n + 1):
            s = abs(m)
            prev = leg[n - 1, s] if n - 1 >= s else np.zeros_like(theta)
            link = math.sqrt((2.0 * n + 1.0) * (n * n - m * m) / (2.0 * n - 1.0))
            pis.append(m * leg[n, s] / sine)
            taus.append((n * cos_theta * leg[n, s] - link * prev) / sine)
            unit = (1.0, -1j, -1.0, 1j)[(n + 1) % 4]
            waves.append(unit * np.exp(1j * m * azimuth) / math.sqrt(n * (n + 1.0)))
    pi, tau, wave = np.stack(pis, 1), np.stack(taus, 1), np.stack(waves, 1)
    wr, wi = wave.real, wave.imag
    polar = np.stack([np.concatenate([pi, tau] * 2, 1), np.concatenate([tau, pi] * 2, 1)])
    azim = np.stack([
        np.concatenate([-wi, wr, -wr, -wi], 1),
        np.concatenate([wr, wi, -wi, wr], 1),
        np.concatenate([-wr, -wi, wi, -wr], 1),
        np.concatenate([-wi, wr, -wr, -wi], 1),
    ])
    return polar, azim, sine


def rotate(table, real, imag):
    half = table.shape[0] // 2
    width = real.shape[1]
    product = jnp.dot(table, jnp.concatenate([real, imag], 1), preferred_element_type=jnp.float32)
    return (
        product[:half, :width] - product[half:, width:],
        product[half:, :width] + product[:half, width:],
    )


def split(value):
    high = value.astype(jnp.bfloat16)
    return high, (value - high.astype(jnp.float32)).astype(jnp.bfloat16)


def far_kernel(
    sph_n, ang_n, coef, pol,
    pos, absorb, det, coef_hbm, table_hbm, inc_hbm, pol_hbm, azi_hbm, amp_hbm, stats,
    coefs, table_x, table_y, table_z, part,    h_in, acc, in_a, in_b, in_z, gath, inc, tpol, tazi, basis_high, basis_low, amp, pow_send, pow_recv,
    s0, r0, sa, ra, sb, rb, sz, rz, ga, gb, gz, rg, s3, r3, s4, r4, lsem, csem, tsem,
):
    n = sph_n * ang_n
    q = ang_n // 2
    nz = sph_n // q
    m = n // 2
    sph, ang = lax.axis_index("sph"), lax.axis_index("ang")
    p = lax.rem(ang, 2)
    x, y, z = lax.rem(sph, q), ang // 2, sph // q
    a = x * (1 - p) + y * p
    b = y * (1 - p) + x * p
    chip = (a * q + b) * nz + z
    me = sph * ang_n + ang
    partner = (sph, ang + 1 - 2 * p)

    def peer(a2, b2, z2):
        x2 = a2 * (1 - p) + b2 * p
        y2 = b2 * (1 - p) + a2 * p
        return (z2 * q + x2, 2 * y2 + p)

    def at(a2, b2, z2):
        return (a2 * q + b2) * nz + z2

    def device(d):
        return (d // ang_n, lax.rem(d, ang_n))

    spheres = coefs.shape[0]
    fields = coefs.shape[2] // 2

    def coef_copy(j):
        return pltpu.make_async_copy(coef_hbm.at[j], coefs.at[j], csem.at[j])

    tables = (table_x, table_y, table_z)

    def table_copy(axis):
        return pltpu.make_async_copy(table_hbm.at[axis], tables[axis], tsem.at[axis])

    table_copy(2).start()
    coef_copy(0).start()
    for j in range(1, spheres):
        coef_copy(j).start()
    table_copy(1).start()
    table_copy(0).start()
    local = [
        pltpu.make_async_copy(inc_hbm, inc, lsem.at[0]),
        pltpu.make_async_copy(pol_hbm.at[sph], tpol, lsem.at[1]),
        pltpu.make_async_copy(azi_hbm.at[ang], tazi, lsem.at[2]),
    ]
    for copy in local:
        copy.start()

    barrier = pltpu.get_barrier_semaphore()

    def greet(k, carry):
        pl.semaphore_signal(
            barrier, inc=1, device_id=device(lax.rem(me + k, n)), device_id_type=MESH
        )
        return carry

    lax.fori_loop(1, n, greet, 0)
    part[...] = jnp.zeros_like(part)
    weight = absorb[...].T
    lanes = lax.broadcasted_iota(jnp.int32, weight.shape, 1)

    def step_first(j, carry):
        coef_copy(j).wait()
        vr, vi = coefs[j, :, :fields], coefs[j, :, fields:]
        wr, wi = vr.astype(jnp.float32), vi.astype(jnp.float32)
        column = jnp.sum(jnp.where(lanes == j, weight, 0.0), axis=1, keepdims=True)
        energy = (wr * wr + wi * wi) * column
        part[2 * coef : 2 * coef + 1, :] += jnp.sum(energy, axis=0, keepdims=True)
        fr, fi = rotate(tables[2][pos[2, j]], vr, vi)
        coefs[j, :, :fields] = fr.astype(jnp.bfloat16)
        coefs[j, :, fields:] = fi.astype(jnp.bfloat16)
        return carry

    def step_second(j, carry):
        fr, fi = rotate(tables[1][pos[1, j]], coefs[j, :, :fields], coefs[j, :, fields:])
        coefs[j, :, :fields] = fr.astype(jnp.bfloat16)
        coefs[j, :, fields:] = fi.astype(jnp.bfloat16)
        return carry

    def step_third(j, carry):
        fr, fi = rotate(tables[0][pos[0, j]], coefs[j, :, :fields], coefs[j, :, fields:])
        part[:coef, :] += fr
        part[coef : 2 * coef, :] += fi
        return carry

    table_copy(2).wait()
    lax.fori_loop(0, spheres, step_first, 0, unroll=2)
    table_copy(1).wait()
    lax.fori_loop(0, spheres, step_second, 0, unroll=4)
    table_copy(0).wait()
    lax.fori_loop(0, spheres, step_third, 0, unroll=4)
    pl.semaphore_wait(barrier, n - 1)

    remote = pltpu.make_async_remote_copy

    r = gath.shape[1]

    def piece_of(c):
        return pl.ds(pl.multiple_of(c * r, 8), r)

    def copy0(c):
        return remote(part.at[piece_of((1 - p) * m + c)], h_in.at[c], s0.at[c], r0.at[c], partner, MESH)

    def send_a(a2, i, src):
        return remote(
            acc.at[a2 * q * nz + i], in_a.at[src * q * nz + i],
            sa.at[a2 * q * nz + i], ra.at[src * q * nz + i], peer(a2, b, z), MESH,
        )

    def send_b(b2, z2, src):
        return remote(
            acc.at[at(a, b2, z2)], in_b.at[src * nz + z2],
            sb.at[b2 * nz + z2], rb.at[src * nz + z2], peer(a, b2, z), MESH,
        )

    def send_z(z2, src):
        return remote(
            acc.at[at(a, b, z2)], in_z.at[src], sz.at[z2], rz.at[src], peer(a, b, z2), MESH
        )

    def spread(c, send, device_id):
        row = gath.at[p * m + c]
        return remote(row, row, send, rg.at[c], device_id, MESH)

    def spread_a(a2, b2, z2):
        return spread(at(a, b2, z2), ga.at[at(a2, b2, z2)], peer(a2, b, z))

    def spread_b(b2, z2):
        return spread(at(a, b, z2), gb.at[b2 * nz + z2], peer(a, b2, z))

    def spread_z(z2):
        return spread(chip, gz.at[z2], peer(a, b, z2))

    def arrived(c):
        spread(c, gz.at[0], partner).wait_recv()

    def copy3(c, half):
        row = gath.at[half * m + c]
        return remote(row, row, s3.at[c], r3.at[c], partner, MESH)

    def copy4(d, slot):
        return pltpu.make_async_remote_copy(
            pow_send.at[lax.rem(d, ang_n)], pow_recv.at[slot], s4.at[d], r4.at[slot], device(d), MESH
        )

    def loop(low, high, body):
        def step(k, carry):
            body(k)
            return carry

        lax.fori_loop(low, high, step, 0)

    def shift(base, k, size):
        return lax.rem(base + k, size)

    loop(1, m + 1, lambda k: copy0(shift(b * q * nz + q * nz - 1, k, m)).start())

    def first(c):
        copy0(c).wait_recv()
        acc[c] = part[piece_of(p * m + c), :] + h_in[c]

    for da in range(1, q):
        a2 = shift(a, da, q)

        def step_a(k):
            i = shift((b + 1) * nz, k, q * nz)
            first(a2 * q * nz + i)
            send_a(a2, i, a).start()

        loop(0, q * nz, step_a)

    def add_a(b2, z2):
        c = at(a, b2, z2)
        first(c)
        value = acc[c]
        for da in range(1, q):
            src = shift(a, da, q)
            send_a(src, b2 * nz + z2, src).wait_recv()
            value = value + in_a[at(src, b2, z2)]
        acc[c] = value

    for db in range(1, q):
        b2 = shift(b, db, q)

        def step_b(k):
            z2 = shift(z, k, nz)
            add_a(b2, z2)
            send_b(b2, z2, b).start()

        loop(1, nz + 1, step_b)

    def add_b(z2):
        add_a(b, z2)
        value = acc[at(a, b, z2)]
        for db in range(1, q):
            src = shift(b, db, q)
            send_b(src, z2, src).wait_recv()
            value = value + in_b[src * nz + z2]
        acc[at(a, b, z2)] = value

    def step_z(k):
        z2 = shift(z, k, nz)
        add_b(z2)
        send_z(z2, z).start()

    loop(1, nz, step_z)
    add_b(z)

    for copy in local:
        copy.wait()
    azi = tazi.shape[1]
    block = pol * azi
    for cr in range(4):
        for i in range(pol):
            rows = slice(cr * block + i * azi, cr * block + (i + 1) * azi)
            high, low = split(tpol[cr // 2, i : i + 1, :] * tazi[cr])
            basis_high[rows, :] = high
            basis_low[rows, :] = low

    def gather_sum(k, total):
        src = shift(z, k, nz)
        send_z(src, src).wait_recv()
        return total + in_z[src]

    gath[p * m + chip] = lax.fori_loop(1, nz, gather_sum, acc[chip])
    loop(1, nz, lambda k: spread_z(shift(z, k, nz)).start())

    def plane(k):
        z2 = shift(z, k, nz)
        if_own = at(a, b, z2)
        for db in range(1, q):
            spread_b(shift(b, db, q), z2).start()
        for da in range(1, q):
            spread_a(shift(a, da, q), b, z2).start()
        copy3(if_own, p).start()

    plane(0)

    def step_plane(k):
        arrived(at(a, b, shift(z, k, nz)))
        plane(k)

    loop(1, nz, step_plane)

    def step_line(k):
        z2 = shift(z, k, nz)
        for db in range(1, q):
            b2 = shift(b, db, q)
            arrived(at(a, b2, z2))
            for da in range(1, q):
                spread_a(shift(a, da, q), b2, z2).start()
            copy3(at(a, b2, z2), p).start()

    loop(0, nz, step_line)

    def step_rest(k):
        for db in range(q):
            for da in range(1, q):
                c = at(shift(a, da, q), shift(b, db, q), shift(z, k, nz))
                arrived(c)
                copy3(c, p).start()

    loop(0, nz, step_rest)
    loop(0, m, lambda k: copy3(k, 1 - p).wait_recv())

    rows = gath.shape[0] * gath.shape[1]
    anchor = gath[...].reshape(rows, fields)
    a_high, a_low = split(anchor[: 2 * coef])
    w_high, w_low = basis_high[:, : 2 * coef], basis_low[:, : 2 * coef]
    dot = functools.partial(jnp.dot, preferred_element_type=jnp.float32)
    both = dot(jnp.concatenate([w_high, w_low], 0), a_high)
    far = both[: 4 * block] + (dot(w_high, a_low) + both[4 * block :])
    amp[...] = far
    out_copy = pltpu.make_async_copy(amp, amp_hbm, lsem.at[0])
    out_copy.start()

    azim_total = det.shape[1]
    want = lax.broadcasted_iota(jnp.int32, (azi, azim_total), 0) + ang * azi
    lane = lax.broadcasted_iota(jnp.int32, (azi, azim_total), 1)
    power = jnp.zeros((1, fields), jnp.float32)
    for i in range(pol):
        weight = jnp.sum(
            jnp.where(lane == want, det[i : i + 1, :], 0.0), axis=1, keepdims=True
        ) * tpol[0, i : i + 1, 2 * coef : 2 * coef + 1]
        total = jnp.zeros((azi, fields), jnp.float32)
        for cr in range(4):
            piece = far[cr * block + i * azi : cr * block + (i + 1) * azi, :]
            total = total + piece * piece
        power = power + jnp.sum(total * weight, axis=0, keepdims=True)
    share = fields // ang_n

    def own(row):
        value = row[:, :share]
        for g in range(1, ang_n):
            value = jnp.where(ang == g, row[:, g * share : (g + 1) * share], value)
        return value

    for g in range(ang_n):
        pow_send[g] = power[:, g * share : (g + 1) * share]
    pow_recv[me] = own(power)
    loop(1, n, lambda k: copy4(lax.rem(me + k, n), me).start())

    stats[0:1, :] = own(jnp.sum(
        inc[:, :fields] * anchor[:coef] + inc[:, fields:] * anchor[coef : 2 * coef],
        axis=0, keepdims=True,
    ))
    stats[1:2, :] = own(anchor[2 * coef : 2 * coef + 1])

    def finish(k):
        copy0(k).wait_send()
        copy3(k, p).wait_send()

    loop(0, m, finish)

    def finish_plane(k):
        for db in range(q):
            b2 = shift(b, db, q)
            for da in range(1, q):
                a2 = shift(a, da, q)
                send_a(a2, b2 * nz + k, a).wait_send()
                spread_a(a2, b2, k).wait_send()
            if db > 0:
                send_b(b2, k, b).wait_send()
                spread_b(b2, k).wait_send()

    loop(0, nz, finish_plane)

    def finish_line(k):
        z2 = shift(z, k, nz)
        send_z(z2, z).wait_send()
        spread_z(z2).wait_send()

    loop(1, nz, finish_line)

    def finish_power(k):
        d = lax.rem(me + k, n)
        copy4(d, d).wait_recv()
        copy4(d, me).wait_send()

    loop(1, n, finish_power)
    stats[2:3, :] = lax.fori_loop(
        1, n, lambda k, total: total + pow_recv[k], pow_recv[0]
    )
    out_copy.wait()


def far_part(positions, absorb_weight, detector, coefficients, shift_tables, incident, polar, azim, sph_n, ang_n):
    n = sph_n * ang_n
    spheres, coef, columns = coefficients.shape
    fields = columns // 2
    r = 8 * -(-(2 * coef + 1) // (8 * n))
    m = n // 2
    nz = sph_n // (ang_n // 2)
    line = n // ang_n
    pol = detector.shape[0]
    azi = azim.shape[2]
    wide = polar.shape[3]
    smem = pl.BlockSpec(memory_space=pltpu.SMEM)
    vmem = pl.BlockSpec(memory_space=pltpu.VMEM)
    hbm = pl.BlockSpec(memory_space=pltpu.HBM)
    f32 = jnp.float32
    dma = pltpu.SemaphoreType.DMA
    return pl.pallas_call(
        functools.partial(far_kernel, sph_n, ang_n, coef, pol),
        out_shape=(
            jax.ShapeDtypeStruct((4 * pol * azi, fields), f32),
            jax.ShapeDtypeStruct((3, fields // ang_n), f32),
        ),
        in_specs=[smem, vmem, vmem, hbm, hbm, hbm, hbm, hbm],
        out_specs=(pl.BlockSpec(memory_space=pl.ANY), vmem),
        scratch_shapes=[
            pltpu.VMEM(coefficients.shape, jnp.bfloat16),
            pltpu.VMEM(shift_tables.shape[1:], jnp.bfloat16),
            pltpu.VMEM(shift_tables.shape[1:], jnp.bfloat16),
            pltpu.VMEM(shift_tables.shape[1:], jnp.bfloat16),
            pltpu.VMEM((n * r, fields), f32),
            pltpu.VMEM((m, r, fields), f32),
            pltpu.VMEM((m, r, fields), f32),
            pltpu.VMEM((m, r, fields), f32),
            pltpu.VMEM((line, r, fields), f32),
            pltpu.VMEM((nz, r, fields), f32),
            pltpu.VMEM((n, r, fields), f32),
            pltpu.VMEM(incident.shape, f32),
            pltpu.VMEM((2, pol, wide), f32),
            pltpu.VMEM((4, azi, wide), f32),
            pltpu.VMEM((4 * pol * azi, wide), jnp.bfloat16),
            pltpu.VMEM((4 * pol * azi, wide), jnp.bfloat16),
            pltpu.VMEM((4 * pol * azi, fields), f32),
            pltpu.VMEM((ang_n, 1, fields // ang_n), f32),
            pltpu.VMEM((n, 1, fields // ang_n), f32),
        ]
        + [dma((size,)) for size in (m, m, m, m, line, line, nz, nz, m, line, nz, m, m, m)]
        + [dma((n,))] * 2
        + [dma((3,)), dma((spheres,)), dma((3,))],
        compiler_params=pltpu.CompilerParams(
            collective_id=0, has_side_effects=True, vmem_limit_bytes=60 * 2**20
        ),
    )(positions.T, absorb_weight, detector, coefficients, shift_tables, incident, polar, azim)


def shards(sph_n, ang_n, coefficients, positions, shift_tables, absorb_weight, incident, detector):
    fields = coefficients.shape[2] // 2
    coef = coefficients.shape[1]
    pol, azim_total = detector.shape
    polar_total = pol * sph_n
    azi = azim_total // ang_n
    order = math.isqrt(coef // 2 + 1) - 1
    wide = 128 * -(-(2 * coef + 1) // 128)
    polar, azim, sine = angular_tables(polar_total, azim_total, order)
    table_polar = np.zeros((sph_n, 2, pol, wide), np.float32)
    table_polar[..., : 2 * coef] = polar.reshape(2, sph_n, pol, 2 * coef).transpose(1, 0, 2, 3)
    solid = 2.0 * math.pi * math.pi / (polar_total * azim_total)
    table_polar[..., 2 * coef] = (sine * solid).reshape(sph_n, 1, pol)
    table_azim = np.zeros((ang_n, 4, azi, wide), np.float32)
    table_azim[..., : 2 * coef] = azim.reshape(4, ang_n, azi, 2 * coef).transpose(1, 0, 2, 3)

    amplitude, stats = far_part(
        positions, absorb_weight, detector, coefficients, shift_tables, incident,
        jnp.asarray(table_polar), jnp.asarray(table_azim), sph_n, ang_n,
    )
    return (amplitude.reshape(2, 2, pol, azi, fields), stats)


def solution(mesh):
    placed = (
        P(("sph", "ang"), None, None),
        P(("sph", "ang"), None),
        P(),
        P(("sph", "ang"), None),
        P(),
        P("sph", None),
    )
    return jax.shard_map(
        functools.partial(shards, mesh.shape["sph"], mesh.shape["ang"]),
        mesh=mesh,
        in_specs=placed,
        out_specs=(P(None, None, "sph", "ang", None), P(None, "ang")),
        check_vma=False,
    )
```
